32 devices in a mesh: groups: 2 (over y), seq: 8 (over z, x), heads: 2 (over core).
Axes of the slice: x: 2, y: 2, z: 4, core: 2. Of those that a mesh axis runs over, the one named last changes fastest.
Arguments:
- queries: bfloat16 [2, 16, 16, 4096], P(None, ('groups', 'seq'), None, 'heads'), parts along dimension 1, may hold values from -8 to 8
- keys: bfloat16 [16, 4096, 512], P(('groups', 'seq'), None, 'heads'), parts along dimension 0, may hold values from -8 to 8
- values: bfloat16 [16, 4096, 512], P(('groups', 'seq'), None, 'heads'), parts along dimension 0, may hold values from -6 to 6
- tile_blocks: int32 [32, 4], P('groups'), parts along dimension 0, may hold values from 0 to 7, all different within a row; in each aligned block of 8 rows (0 to 7, 8 to 15, ...) at most 8 rows name the same one
- block_place: int32 [16], P('groups'), parts along dimension 0, may hold values from 0 to 7, each once
- tile_offset: int32 [32], P('groups'), parts along dimension 0, may hold values from 0 to 255
Outputs:
- attended: bfloat16 [2, 16, 16, 4096], P(None, ('groups', 'seq'), None, 'heads'), parts along dimension 1
The draws below stay inside these ranges and needn't reach their ends.
There are 2 independent parts, one for each index of `groups`. The reference program is written for one: setup_inputs(seed, part) draws one part's arguments, and reference() takes and returns one part's arrays. A program takes and returns all parts, laid end to end along the dimension named above; each array names one. Nothing has to cross between parts.
Inputs may be any that keep to these rules, and one draw needn't show every extreme that they name: `tile_blocks`: each tile lists 4 different blocks; among the 8 tiles of one micro-batch no block is listed by more than 8 tiles, and in some micro-batch one block is listed by exactly 8. `block_place`: each index appears once.
All inputs are finite; a program needn't handle non-finite values.
Results may differ from the reference program's by a relative error of at most 0.0048.
Values may be sent and summed in bfloat16 or wider, within the bound.
A program may use at most 128 MiB of HBM per device.

```python
import math
import jax
import jax.numpy as jnp
import numpy as np
from jax import lax

HEAD = 128
QHEADS = 32
KV_HEADS = 4
TILE = 16
BLOCK = 4096
TOP = 4
MB = 2
TILES_MB = 8
TILES = 16
BLOCKS = 8
GROUP = 8
KF = 512
MOST = 8


def draw_queries(key, part):
    sample = jax.random.normal(jax.random.fold_in(key, 11), (MB, TILES_MB, TILE, QHEADS, HEAD), jnp.float32)
    return jnp.clip(sample, -8.0, 8.0).reshape(MB, TILES_MB, TILE, QHEADS * HEAD).astype(jnp.bfloat16)


def draw_keys(key, part):
    sample = jax.random.normal(jax.random.fold_in(key, 21), (BLOCKS, BLOCK, KV_HEADS, HEAD), jnp.float32)
    return jnp.clip(sample, -8.0, 8.0).reshape(BLOCKS, BLOCK, KV_HEADS * HEAD).astype(jnp.bfloat16)


def plant(entries, key, smallest, largest):
    extent = entries.shape
    index_at = [jax.random.randint(jax.random.fold_in(key, axis), (), 0, extent[axis]) for axis in range(len(extent))]
    entries = entries.at[tuple(index_at)].set(smallest)
    longest = extent.index(max(extent))
    index_at[longest] = (index_at[longest] + 1) % extent[longest]
    return entries.at[tuple(index_at)].set(largest)


def block_levels(rng, shape, cuts, low, top_value):
    def one(dim, blocks):
        draws = jax.random.uniform(jax.random.fold_in(jax.random.fold_in(rng, 6), dim), (blocks,), jnp.float32, low / len(cuts), top_value / len(cuts))
        return jnp.repeat(jnp.exp(draws), shape[dim] // blocks).reshape((-1,) + (1,) * (len(shape) - dim - 1))

    loudness = one(*cuts[0])
    for cut in cuts[1:]:
        loudness = loudness * one(*cut)
    return loudness


def routed_block(key, own, number, rows, number_of, top, most, slope):
    order = jax.random.permutation(key, number_of)
    packed, ordinary = load_shares(number_of, rows * top, most, slope, True), load_shares(number_of, rows * top, most, slope, False)
    places = jnp.arange(number_of)

    def named(tallies, rotation):
        used = int((tallies > 0).sum())
        fixed = max(1, used // 4)
        shifted = fixed + (places - fixed + rotation * (used - fixed)) % max(1, number_of - fixed)
        return jnp.zeros((number_of,), jnp.int32).at[order[jnp.where(places < fixed, places, shifted)]].set(jnp.asarray(tallies, jnp.int32))

    tallies = jnp.where(number % 4 == 0, named(packed, number // 4), named(ordinary, number - number // 4 - 1))
    mixed = jax.random.permutation(jax.random.fold_in(own, 3), number_of)
    source_of, taker = mixed[0:number_of // 2 * 2:2], mixed[1:number_of // 2 * 2:2]
    slack = jnp.minimum(tallies[source_of] - 1, most - tallies[taker]) // 2
    slack = jnp.where((source_of == order[0]) | (taker == order[0]) | (tallies[taker] == 0), 0, jnp.maximum(slack, 0))
    shifted = jax.random.randint(jax.random.fold_in(own, 4), (number_of // 2,), 0, 1 << 20) % (slack + 1)
    tallies = tallies.at[source_of].add(-shifted).at[taker].add(shifted)
    items = jnp.searchsorted(jnp.cumsum(tallies), jnp.arange(rows * top), side="right").astype(jnp.int32)
    grid = items.reshape(top, rows).T
    grid = grid[jax.random.permutation(jax.random.fold_in(own, 1), rows)]
    rotation = jax.random.randint(jax.random.fold_in(own, 2), (rows, 1), 0, top)
    return jnp.take_along_axis(grid, (jnp.arange(top)[None, :] + rotation) % top, axis=1)


def load_shares(count, total, bound, skew, full):
    weights = [(1 << 20) // math.isqrt(standing ** skew) + 1 for standing in range(1, count + 1)]
    largest = bound if full else min(bound, max(-(-total // count), total * weights[0] // sum(weights)))
    least = 1 if total - largest >= count - 1 else 0
    given, rest = [largest] + [least] * (count - 1), total - largest - least * (count - 1)
    while rest > 0:
        movable = [i for i in range(1, count) if given[i] < largest] or [i for i in range(1, count) if given[i] < bound]
        pool, budget = sum([weights[i] for i in movable]), rest
        for i in movable:
            extra = min(bound - given[i], max(1, budget * weights[i] // pool), rest)
            given[i] = given[i] + extra
            rest = rest - extra
    return np.array(given)


def gaussian(key, shape, scale, most, cuts=(), held_as=jnp.bfloat16):
    values = scale * jax.random.normal(key, shape, jnp.float32)
    if cuts:
        values = values * block_levels(key, shape, cuts, -0.22, 0.18)
    return jnp.clip(values, -most, most).astype(held_as)


def setup_inputs(seed: int = 0, part: int = 0) -> dict:
    seeds = jax.random.split(jax.random.key(seed), 7)
    own_keys = jax.random.split(jax.random.fold_in(seeds[6], part), 7)
    queries = draw_queries(jax.random.fold_in(jax.random.fold_in(seeds[6], part), 71), part)
    keys = draw_keys(jax.random.fold_in(jax.random.fold_in(seeds[6], part), 71), part)
    values = gaussian(own_keys[2], (BLOCKS, BLOCK, KF), 1.0, 6.0, ((0, 8), (2, 2)))
    tile_blocks_keys = jax.random.split(jax.random.fold_in(own_keys[3], 1), TILES // TILES_MB)
    tile_blocks_turns = jax.random.permutation(jax.random.fold_in(own_keys[3], 3), TILES // TILES_MB)
    tile_blocks = jax.vmap(lambda own, number: routed_block(jax.random.fold_in(own_keys[3], 2), own, number, TILES_MB, BLOCKS, TOP, MOST, 2))(tile_blocks_keys, tile_blocks_turns).reshape((TILES, TOP))
    block_place = jax.random.permutation(own_keys[4], BLOCKS).astype(jnp.int32)
    tile_offset = plant(jax.random.randint(own_keys[5], (TILES,), 0, BLOCK // TILE), jax.random.fold_in(own_keys[5], 1), 0, (BLOCK // TILE) - 1).astype(jnp.int32)
    return {"queries": queries, "keys": keys, "values": values, "tile_blocks": tile_blocks, "block_place": block_place, "tile_offset": tile_offset}


def partial_block(tile_query, key_block, value_block, horizon):
    scores = jnp.einsum('rcgh,kch->cgrk', tile_query.astype(jnp.float32), key_block.astype(jnp.float32)) * HEAD ** -0.5
    visible = jnp.arange(BLOCK, dtype=jnp.int32)[None, :] <= horizon[:, None]
    scores = jnp.where(visible[None, None], scores, -1e30)
    highest = jnp.max(scores, axis=3, keepdims=True)
    weights = jnp.exp(scores - highest)
    summed = jnp.sum(weights, axis=3, keepdims=True)
    rounded = lax.optimization_barrier(weights.astype(jnp.bfloat16)).astype(jnp.float32)
    blended = jnp.einsum('cgrk,kch->cgrh', rounded, value_block.astype(jnp.float32)) / summed
    return blended, (highest + jnp.log(summed))[..., 0]


def reference(queries, keys, values, tile_blocks, block_place, tile_offset):
    tile_count = queries.shape[0] * queries.shape[1]
    shaped = queries.reshape(tile_count, TILE, KV_HEADS, GROUP, HEAD)
    key_blocks = keys.reshape(keys.shape[0], BLOCK, KV_HEADS, HEAD)
    value_blocks = values.reshape(values.shape[0], BLOCK, KV_HEADS, HEAD)

    def one_tile(bundle):
        tile_query, block_list, offset = bundle
        own_block = jnp.max(block_list)
        horizon_own = (offset * TILE + jnp.arange(TILE, dtype=jnp.int32)).astype(jnp.int32)
        pieces = []
        masses = []
        for entry_index in range(TOP):
            owner_row = block_place[block_list[entry_index]]
            horizon = jnp.where(block_list[entry_index] == own_block, horizon_own, BLOCK).astype(jnp.int32)
            blended, mass = partial_block(tile_query, key_blocks[owner_row], value_blocks[owner_row], horizon)
            pieces.append(blended)
            masses.append(mass)
        stacked = jnp.stack(pieces)
        mass_all = jnp.stack(masses)
        highest = jnp.max(mass_all, axis=0, keepdims=True)
        share_all = jnp.exp(mass_all - highest)
        share_all = share_all / jnp.sum(share_all, axis=0, keepdims=True)
        result = jnp.sum(share_all[..., None] * stacked, axis=0)
        return result.transpose(2, 0, 1, 3).reshape(TILE, KV_HEADS * GROUP * HEAD).astype(jnp.bfloat16)

    output = lax.map(one_tile, (shaped, tile_blocks, tile_offset))
    return output.reshape(queries.shape)
```

```python
import functools
import math

import jax
import jax.numpy as jnp
from jax import lax
from jax.experimental import pallas as pl
from jax.experimental.pallas import tpu as pltpu
from jax.sharding import PartitionSpec as P

HEAD = 128
CHUNK = 1024
MASKED = -1e30
RATE = HEAD ** (-0.5) * math.log2(math.e)
MESH = pl.DeviceIdType.MESH
F32 = jnp.float32
BF16 = jnp.bfloat16


def dot_t(a, b):
    return lax.dot_general(a, b, (((1,), (1,)), ((), ())), preferred_element_type=F32)


def kernel(
    n, block_ref, place_ref, offset_ref, q_hbm, k_hbm, v_hbm, out_ref,
    qbuf, kbuf, vbuf, masks, s0, s1, m0, m1, sbuf, rbuf, mass_s, mass_r, shares,
    kv_sem, q_local, q_send, q_recv, r_send, r_recv, c_send, c_recv,
):
    me = lax.axis_index("seq")
    batch, _, rows, features = q_hbm.shape
    block = k_hbm.shape[1]
    shared = k_hbm.shape[2] // HEAD
    group = features // k_hbm.shape[2]
    top = block_ref.shape[1]
    tile = group * rows
    total = batch * tile
    chunks = block // CHUNK
    scores = (s0, s1)
    peaks = (m0, m1)

    def distance(k):
        return k

    loads = []
    for c in range(shared):
        columns = pl.ds(c * HEAD, HEAD)
        loads.append((
            pltpu.make_async_copy(k_hbm.at[0, :, columns], kbuf.at[c], kv_sem.at[0, c]),
            pltpu.make_async_copy(v_hbm.at[0, :, columns], vbuf.at[c], kv_sem.at[1, c]),
        ))
    own_query = pltpu.make_async_copy(q_hbm.at[:, 0], qbuf.at[0], q_local.at[0])
    own_query.start()
    for c in range(shared):
        loads[c][0].start()
    for c in range(shared):
        loads[c][1].start()

    barrier = pltpu.get_barrier_semaphore()

    @pl.loop(1, n)
    def _(d):
        pl.semaphore_signal(barrier, inc=1, device_id={"seq": lax.rem(me + d, n)}, device_id_type=MESH)

    pl.semaphore_wait(barrier, n - 1)

    def query_copy(d):
        return pltpu.make_async_remote_copy(
            src_ref=q_hbm.at[:, 0], dst_ref=qbuf.at[n - d], send_sem=q_send.at[d], recv_sem=q_recv.at[n - d],
            device_id={"seq": lax.rem(me + d, n)}, device_id_type=MESH)

    def result_copy(d):
        return pltpu.make_async_remote_copy(
            src_ref=sbuf.at[d], dst_ref=rbuf.at[n - d], send_sem=r_send.at[d], recv_sem=r_recv.at[n - d],
            device_id={"seq": lax.rem(me + d, n)}, device_id_type=MESH)

    def mass_copy(d):
        return pltpu.make_async_remote_copy(
            src_ref=mass_s.at[d], dst_ref=mass_r.at[n - d], send_sem=c_send.at[d], recv_sem=c_recv.at[n - d],
            device_id={"seq": lax.rem(me + d, n)}, device_id_type=MESH)

    def query_arrival(d):
        return pltpu.make_async_remote_copy(
            src_ref=q_hbm.at[:, 0], dst_ref=qbuf.at[d], send_sem=q_send.at[d], recv_sem=q_recv.at[d],
            device_id={"seq": lax.rem(me + d, n)}, device_id_type=MESH)

    def result_arrival(d):
        return pltpu.make_async_remote_copy(
            src_ref=sbuf.at[d], dst_ref=rbuf.at[d], send_sem=r_send.at[d], recv_sem=r_recv.at[d],
            device_id={"seq": lax.rem(me + d, n)}, device_id_type=MESH)

    def mass_arrival(d):
        return pltpu.make_async_remote_copy(
            src_ref=mass_s.at[d], dst_ref=mass_r.at[d], send_sem=c_send.at[d], recv_sem=c_recv.at[d],
            device_id={"seq": lax.rem(me + d, n)}, device_id_type=MESH)

    @pl.loop(1, n)
    def _(k):
        query_copy(distance(k)).start()

    my_block = lax.fori_loop(
        0, place_ref.shape[0], lambda e, found: found + jnp.where(place_ref[e] == me, e, 0), jnp.int32(0))
    lanes = lax.broadcasted_iota(jnp.int32, (1, HEAD), 1)
    tile_lane = lax.broadcasted_iota(jnp.int32, (tile, HEAD), 1)
    tile_row = lax.rem(lax.broadcasted_iota(jnp.int32, (tile, HEAD), 0), rows)

    def first_hidden(d):
        hidden = jnp.zeros((1, HEAD), jnp.int32)
        for b in range(batch):
            t = b * n + lax.rem(me + d, n)
            entries = [block_ref[t, e] for e in range(top)]
            own = functools.reduce(jnp.maximum, entries)
            hits = functools.reduce(lambda x, y: x + y, [jnp.where(e == my_block, 1, 0) for e in entries])
            start = jnp.where(own == my_block, offset_ref[t] * rows, jnp.where(hits > 0, block, -2 * rows))
            column = lanes - b * rows
            hidden = jnp.where((column >= 0) & (column < rows), start + column + 1, hidden)
        return hidden

    def query_rows(d, c):
        parts = []
        for b in range(batch):
            piece = jnp.concatenate(
                [qbuf[d, b, :, pl.ds((c * group + g) * HEAD, HEAD)] for g in range(group)], axis=0)
            mark = jnp.where(tile_lane == tile_row + b * rows, MASKED, 0.0).astype(BF16)
            parts.append(jnp.concatenate([piece, mark], axis=1))
        return jnp.concatenate(parts, axis=0)

    def both(fresh, ready):
        if fresh is not None:
            d_new, c_new = fresh
            query = query_rows(d_new, c_new)
            peak = None
            if c_new == 0:
                hidden = first_hidden(d_new)
        if ready is not None:
            d_old, c_old = ready
            top_score = jnp.max(peaks[c_old][...], axis=1, keepdims=True)
            blend = jnp.zeros((total, 2 * HEAD), F32)
        for j in range(chunks):
            here = slice(j * CHUNK, (j + 1) * CHUNK)
            if fresh is not None:
                if c_new == 0:
                    position = lax.broadcasted_iota(jnp.int32, (CHUNK, HEAD), 0) + j * CHUNK
                    mask = jnp.where(position >= hidden, 1.0, 0.0).astype(BF16)
                    masks[here, :] = mask
                else:
                    mask = masks[here, :]
                part = dot_t(query, jnp.concatenate([kbuf[c_new, here, :], mask], axis=1))
                scores[c_new][:, here] = part
                for i in range(CHUNK // HEAD):
                    column = part[:, i * HEAD:(i + 1) * HEAD]
                    peak = column if peak is None else jnp.maximum(peak, column)
            if ready is not None:
                weights = jnp.exp2((scores[c_old][:, here] - top_score) * RATE).astype(BF16)
                value = jnp.concatenate([vbuf[c_old, here, :], jnp.ones((CHUNK, HEAD), BF16)], axis=1)
                blend = blend + jnp.dot(weights, value, preferred_element_type=F32)
        if fresh is not None:
            peaks[c_new][...] = peak
        if ready is not None:
            summed = blend[:, HEAD:]
            result = (blend[:, :HEAD] / summed).astype(BF16)
            mass = jnp.log2(summed) + top_score * RATE
            head_lane = lax.broadcasted_iota(jnp.int32, (rows, HEAD), 1)
            for b in range(batch):
                kept = jnp.zeros((rows, HEAD), F32) if c_old == 0 else mass_s[d_old, b]
                for g in range(group):
                    span = slice(b * tile + g * rows, b * tile + (g + 1) * rows)
                    head = c_old * group + g
                    sbuf[d_old, b, :, pl.ds(head * HEAD, HEAD)] = result[span]
                    kept = jnp.where(head_lane == head, mass[span], kept)
                mass_s[d_old, b] = kept

    own_query.wait()
    for c in range(shared):
        loads[c][0].wait()
        loads[c][1].wait()
    both((0, 0), None)

    def finish(d):
        result_copy(d).start()
        mass_copy(d).start()

    @pl.loop(0, n - 1)
    def _(k):
        d, later = distance(k), distance(k + 1)
        both((d, 1), (d, 0))
        query_arrival(later).wait_recv()
        both((later, 0), (d, 1))

        @pl.when(k > 0)
        def _():
            finish(d)

    last = distance(n - 1)
    both((last, 1), (last, 0))
    both(None, (last, 1))
    finish(last)

    @pl.loop(1, n)
    def _(d):
        mass_arrival(d).wait_recv()

    highest = mass_s[0]
    for_all = lambda f, init: lax.fori_loop(1, n, f, init)
    highest = for_all(lambda d, m: jnp.maximum(m, mass_r[d]), highest)
    bottom = for_all(lambda d, s: s + jnp.exp2(mass_r[d] - highest), jnp.exp2(mass_s[0] - highest))

    @pl.loop(1, n)
    def _(d):
        result_arrival(d).wait_recv()

    shares[0] = jnp.exp2(mass_s[0] - highest) / bottom

    @pl.loop(1, n)
    def _(d):
        shares[d] = jnp.exp2(mass_r[d] - highest) / bottom

    for b in range(batch):
        for head in range(shared * group):
            columns = pl.ds(head * HEAD, HEAD)

            def add(d, sofar):
                return sofar + shares[d, b][:, head:head + 1] * rbuf[d, b, :, columns].astype(F32)

            value = shares[0, b][:, head:head + 1] * sbuf[0, b, :, columns].astype(F32)
            out_ref[b, 0, :, columns] = lax.fori_loop(1, n, add, value, unroll=n <= 8).astype(BF16)

    @pl.loop(1, n)
    def _(d):
        query_copy(d).wait_send()
        result_copy(d).wait_send()
        mass_copy(d).wait_send()


def local(n, queries, keys, values, tile_blocks, block_place, tile_offset):
    batch, _, rows, features = queries.shape
    block = keys.shape[1]
    shared = keys.shape[2] // HEAD
    group = features // keys.shape[2]
    total = batch * group * rows
    smem = pl.BlockSpec(memory_space=pltpu.SMEM)
    far = pl.BlockSpec(memory_space=pl.ANY)
    dma = pltpu.SemaphoreType.DMA
    return pl.pallas_call(
        functools.partial(kernel, n),
        out_shape=jax.ShapeDtypeStruct(queries.shape, queries.dtype),
        in_specs=[smem, smem, smem, far, far, far],
        out_specs=pl.BlockSpec(memory_space=pltpu.VMEM),
        scratch_shapes=[
            pltpu.VMEM((n, batch, rows, features), BF16),
            pltpu.VMEM((shared, block, HEAD), BF16),
            pltpu.VMEM((shared, block, HEAD), BF16),
            pltpu.VMEM((block, HEAD), BF16),
            pltpu.VMEM((total, block), F32),
            pltpu.VMEM((total, block), F32),
            pltpu.VMEM((total, HEAD), F32),
            pltpu.VMEM((total, HEAD), F32),
            pltpu.VMEM((n, batch, rows, features), BF16),
            pltpu.VMEM((n, batch, rows, features), BF16),
            pltpu.VMEM((n, batch, rows, HEAD), F32),
            pltpu.VMEM((n, batch, rows, HEAD), F32),
            pltpu.VMEM((n, batch, rows, HEAD), F32),
            dma((2, shared)),
            dma((1,)),
            dma((n,)), dma((n,)), dma((n,)), dma((n,)), dma((n,)), dma((n,)),
        ],
        compiler_params=pltpu.CompilerParams(
            collective_id=0, has_side_effects=True, vmem_limit_bytes=60 * 1024 * 1024),
    )(tile_blocks, block_place, tile_offset, queries, keys, values)


def solution(mesh):
    placed = (
        P(None, ("groups", "seq"), None, "heads"),
        P(("groups", "seq"), None, "heads"),
        P(("groups", "seq"), None, "heads"),
        P("groups", None),
        P("groups"),
        P("groups"),
    )
    return jax.shard_map(
        functools.partial(local, mesh.shape["seq"]),
        mesh=mesh,
        in_specs=placed,
        out_specs=P(None, ("groups", "seq"), None, "heads"),
        check_vma=False,
    )
```

```python
import functools
import math

import jax
import jax.numpy as jnp
from jax import lax
from jax.experimental import pallas as pl
from jax.experimental.pallas import tpu as pltpu
from jax.sharding import PartitionSpec as P

HEAD = 128
CHUNK = 1024
MASKED = -1e30
RATE = HEAD ** (-0.5) * math.log2(math.e)
MESH = pl.DeviceIdType.MESH
F32 = jnp.float32
BF16 = jnp.bfloat16


def dot_t(a, b):
    return lax.dot_general(a, b, (((1,), (1,)), ((), ())), preferred_element_type=F32)


def kernel(
    n, block_ref, place_ref, offset_ref, q_hbm, k_hbm, v_hbm, out_ref,
    qbuf, kbuf, vbuf, masks, s0, s1, m0, m1, sbuf, mass_s, xbuf, mass_x, gbuf, mass_g, rbuf, mass_r, shares,
    kv_sem, q_local, q_send, q_recv, f_send, f_recv, x_send, x_recv, y_send, y_recv, r_send, r_recv, c_send, c_recv,
):
    me = lax.axis_index("seq")
    batch, _, rows, features = q_hbm.shape
    block = k_hbm.shape[1]
    shared = k_hbm.shape[2] // HEAD
    group = features // k_hbm.shape[2]
    top = block_ref.shape[1]
    tile = group * rows
    total = batch * tile
    chunks = block // CHUNK
    scores = (s0, s1)
    peaks = (m0, m1)

    lines = n // 2
    line, side = me // 2, lax.rem(me, 2)

    def device(j, p):
        return lax.rem(line + j, lines) * 2 + lax.rem(side + p, 2)

    loads = []
    for c in range(shared):
        columns = pl.ds(c * HEAD, HEAD)
        loads.append((
            pltpu.make_async_copy(k_hbm.at[0, :, columns], kbuf.at[c], kv_sem.at[0, c]),
            pltpu.make_async_copy(v_hbm.at[0, :, columns], vbuf.at[c], kv_sem.at[1, c]),
        ))
    own_query = pltpu.make_async_copy(q_hbm.at[:, 0], qbuf.at[0], q_local.at[0])
    own_query.start()
    for c in range(shared):
        loads[c][0].start()
    for c in range(shared):
        loads[c][1].start()

    barrier = pltpu.get_barrier_semaphore()

    def greet(target):
        pl.semaphore_signal(barrier, inc=1, device_id={"seq": target}, device_id_type=MESH)

    greet(device(0, 1))

    @pl.loop(1, lines)
    def _(j):
        greet(device(j, 0))

    pl.semaphore_wait(barrier, lines)

    def remote(src, dst, send, recv, target):
        return pltpu.make_async_remote_copy(
            src_ref=src, dst_ref=dst, send_sem=send, recv_sem=recv,
            device_id={"seq": target}, device_id_type=MESH)

    def query_copy(j, there):
        return remote(q_hbm.at[:, 0], qbuf.at[2 * there], q_send.at[j], q_recv.at[there], device(j, 0))

    def forward_copy(j):
        return remote(qbuf.at[2 * j], qbuf.at[2 * j + 1], f_send.at[j], f_recv.at[j], device(0, 1))

    def cross_copies(j):
        return (remote(sbuf.at[2 * j + 1], xbuf.at[j], x_send.at[j], x_recv.at[j], device(0, 1)),
                remote(mass_s.at[2 * j + 1], mass_x.at[j], y_send.at[j], y_recv.at[j], device(0, 1)))

    def return_copies(j, there):
        return (remote(gbuf.at[j], rbuf.at[there], r_send.at[j], r_recv.at[there], device(j, 0)),
                remote(mass_g.at[j], mass_r.at[there], c_send.at[j], c_recv.at[there], device(j, 0)))

    @pl.loop(1, lines)
    def _(j):
        query_copy(j, lines - j).start()

    own_query.wait()
    forward_copy(0).start()

    my_block = lax.fori_loop(
        0, place_ref.shape[0], lambda e, found: found + jnp.where(place_ref[e] == me, e, 0), jnp.int32(0))
    lanes = lax.broadcasted_iota(jnp.int32, (1, HEAD), 1)
    tile_lane = lax.broadcasted_iota(jnp.int32, (tile, HEAD), 1)
    tile_row = lax.rem(lax.broadcasted_iota(jnp.int32, (tile, HEAD), 0), rows)

    def first_hidden(d):
        hidden = jnp.zeros((1, HEAD), jnp.int32)
        for b in range(batch):
            t = b * n + device(d // 2, lax.rem(d, 2))
            entries = [block_ref[t, e] for e in range(top)]
            own = functools.reduce(jnp.maximum, entries)
            hits = functools.reduce(lambda x, y: x + y, [jnp.where(e == my_block, 1, 0) for e in entries])
            start = jnp.where(own == my_block, offset_ref[t] * rows, jnp.where(hits > 0, block, -2 * rows))
            column = lanes - b * rows
            hidden = jnp.where((column >= 0) & (column < rows), start + column + 1, hidden)
        return hidden

    def query_rows(d, c):
        parts = []
        for b in range(batch):
            piece = jnp.concatenate(
                [qbuf[d, b, :, pl.ds((c * group + g) * HEAD, HEAD)] for g in range(group)], axis=0)
            mark = jnp.where(tile_lane == tile_row + b * rows, MASKED, 0.0).astype(BF16)
            parts.append(jnp.concatenate([piece, mark], axis=1))
        return jnp.concatenate(parts, axis=0)

    def both(fresh, ready):
        if fresh is not None:
            d_new, c_new = fresh
            query = query_rows(d_new, c_new)
            peak = None
            if c_new == 0:
                hidden = first_hidden(d_new)
        if ready is not None:
            d_old, c_old = ready
            top_score = jnp.max(peaks[c_old][...], axis=1, keepdims=True)
            blend = jnp.zeros((total, 2 * HEAD), F32)
        for j in range(chunks):
            here = slice(j * CHUNK, (j + 1) * CHUNK)
            if fresh is not None:
                if c_new == 0:
                    position = lax.broadcasted_iota(jnp.int32, (CHUNK, HEAD), 0) + j * CHUNK
                    mask = jnp.where(position >= hidden, 1.0, 0.0).astype(BF16)
                    masks[here, :] = mask
                else:
                    mask = masks[here, :]
                part = dot_t(query, jnp.concatenate([kbuf[c_new, here, :], mask], axis=1))
                scores[c_new][:, here] = part
                for i in range(CHUNK // HEAD):
                    column = part[:, i * HEAD:(i + 1) * HEAD]
                    peak = column if peak is None else jnp.maximum(peak, column)
            if ready is not None:
                weights = jnp.exp2((scores[c_old][:, here] - top_score) * RATE).astype(BF16)
                value = jnp.concatenate([vbuf[c_old, here, :], jnp.ones((CHUNK, HEAD), BF16)], axis=1)
                blend = blend + jnp.dot(weights, value, preferred_element_type=F32)
        if fresh is not None:
            peaks[c_new][...] = peak
        if ready is not None:
            summed = blend[:, HEAD:]
            result = (blend[:, :HEAD] / summed).astype(BF16)
            mass = jnp.log2(summed) + top_score * RATE
            head_lane = lax.broadcasted_iota(jnp.int32, (rows, HEAD), 1)
            for b in range(batch):
                kept = jnp.zeros((rows, HEAD), F32) if c_old == 0 else mass_s[d_old, b]
                for g in range(group):
                    span = slice(b * tile + g * rows, b * tile + (g + 1) * rows)
                    head = c_old * group + g
                    sbuf[d_old, b, :, pl.ds(head * HEAD, HEAD)] = result[span]
                    kept = jnp.where(head_lane == head, mass[span], kept)
                mass_s[d_old, b] = kept

    for c in range(shared):
        loads[c][0].wait()
        loads[c][1].wait()
    both((0, 0), None)

    def merge(j):
        for copy in cross_copies(j):
            copy.wait_recv()
        for b in range(batch):
            mine, other = mass_s[2 * j, b], mass_x[j, b]
            highest = jnp.maximum(mine, other)
            first, second = jnp.exp2(mine - highest), jnp.exp2(other - highest)
            bottom = first + second
            mass_g[j, b] = highest + jnp.log2(bottom)
            first, second = first / bottom, second / bottom
            for head in range(shared * group):
                columns = pl.ds(head * HEAD, HEAD)
                gbuf[j, b, :, columns] = (
                    first[:, head:head + 1] * sbuf[2 * j, b, :, columns].astype(F32)
                    + second[:, head:head + 1] * xbuf[j, b, :, columns].astype(F32)).astype(BF16)

    def finish(j):
        merge(j)

        @pl.when(j > 0)
        def _():
            for copy in return_copies(j, lines - j):
                copy.start()

    def step(j, more):
        near, far = 2 * j, 2 * j + 1
        both((near, 1), (near, 0))
        forward_copy(j).wait_recv()
        both((far, 0), (near, 1))
        if more:
            query_copy(j + 1, j + 1).wait_recv()
            forward_copy(j + 1).start()
        both((far, 1), (far, 0))
        both((2 * j + 2, 0) if more else None, (far, 1))
        for copy in cross_copies(j):
            copy.start()

    @pl.loop(0, lines - 1)
    def _(j):
        step(j, True)

        @pl.when(j > 0)
        def _():
            finish(j - 1)

    step(lines - 1, False)
    if lines > 1:
        finish(lines - 2)
    finish(lines - 1)

    @pl.loop(1, lines)
    def _(j):
        for copy in return_copies(j, j):
            copy.wait_recv()

    for_all = lambda f, init: lax.fori_loop(1, lines, f, init)
    highest = for_all(lambda j, m: jnp.maximum(m, mass_r[j]), mass_g[0])
    bottom = for_all(lambda j, total_: total_ + jnp.exp2(mass_r[j] - highest), jnp.exp2(mass_g[0] - highest))
    shares[0] = jnp.exp2(mass_g[0] - highest) / bottom

    @pl.loop(1, lines)
    def _(j):
        shares[j] = jnp.exp2(mass_r[j] - highest) / bottom

    for b in range(batch):
        for head in range(shared * group):
            columns = pl.ds(head * HEAD, HEAD)

            def add(j, sofar):
                return sofar + shares[j, b][:, head:head + 1] * rbuf[j, b, :, columns].astype(F32)

            value = shares[0, b][:, head:head + 1] * gbuf[0, b, :, columns].astype(F32)
            out_ref[b, 0, :, columns] = lax.fori_loop(1, lines, add, value, unroll=n <= 8).astype(BF16)

    @pl.loop(0, lines)
    def _(j):
        forward_copy(j).wait_send()
        for copy in cross_copies(j):
            copy.wait_send()

    @pl.loop(1, lines)
    def _(j):
        query_copy(j, j).wait_send()
        for copy in return_copies(j, j):
            copy.wait_send()


def local(n, queries, keys, values, tile_blocks, block_place, tile_offset):
    batch, _, rows, features = queries.shape
    block = keys.shape[1]
    shared = keys.shape[2] // HEAD
    group = features // keys.shape[2]
    total = batch * group * rows
    lines = n // 2
    smem = pl.BlockSpec(memory_space=pltpu.SMEM)
    far = pl.BlockSpec(memory_space=pl.ANY)
    dma = pltpu.SemaphoreType.DMA
    return pl.pallas_call(
        functools.partial(kernel, n),
        out_shape=jax.ShapeDtypeStruct(queries.shape, queries.dtype),
        in_specs=[smem, smem, smem, far, far, far],
        out_specs=pl.BlockSpec(memory_space=pltpu.VMEM),
        scratch_shapes=[
            pltpu.VMEM((n, batch, rows, features), BF16),
            pltpu.VMEM((shared, block, HEAD), BF16),
            pltpu.VMEM((shared, block, HEAD), BF16),
            pltpu.VMEM((block, HEAD), BF16),
            pltpu.VMEM((total, block), F32),
            pltpu.VMEM((total, block), F32),
            pltpu.VMEM((total, HEAD), F32),
            pltpu.VMEM((total, HEAD), F32),
            pltpu.VMEM((n, batch, rows, features), BF16),
            pltpu.VMEM((n, batch, rows, HEAD), F32),
            pltpu.VMEM((lines, batch, rows, features), BF16),
            pltpu.VMEM((lines, batch, rows, HEAD), F32),
            pltpu.VMEM((lines, batch, rows, features), BF16),
            pltpu.VMEM((lines, batch, rows, HEAD), F32),
            pltpu.VMEM((lines, batch, rows, features), BF16),
            pltpu.VMEM((lines, batch, rows, HEAD), F32),
            pltpu.VMEM((lines, batch, rows, HEAD), F32),
            dma((2, shared)),
            dma((1,)),
            *[dma((lines,))] * 12,
        ],
        compiler_params=pltpu.CompilerParams(
            collective_id=0, has_side_effects=True, vmem_limit_bytes=60 * 1024 * 1024),
    )(tile_blocks, block_place, tile_offset, queries, keys, values)


def solution(mesh):
    placed = (
        P(None, ("groups", "seq"), None, "heads"),
        P(("groups", "seq"), None, "heads"),
        P(("groups", "seq"), None, "heads"),
        P("groups", None),
        P("groups"),
        P("groups"),
    )
    return jax.shard_map(
        functools.partial(local, mesh.shape["seq"]),
        mesh=mesh,
        in_specs=placed,
        out_specs=P(None, ("groups", "seq"), None, "heads"),
        check_vma=False,
    )
```

```python
import functools
import math

import jax
import jax.numpy as jnp
from jax import lax
from jax.experimental import pallas as pl
from jax.experimental.pallas import tpu as pltpu
from jax.sharding import PartitionSpec as P

HEAD = 128
CHUNK = 1024
MASKED = -1e30
RATE = HEAD ** (-0.5) * math.log2(math.e)
MESH = pl.DeviceIdType.MESH
F32 = jnp.float32
BF16 = jnp.bfloat16


def dot_t(a, b):
    return lax.dot_general(a, b, (((1,), (1,)), ((), ())), preferred_element_type=F32)


def kernel(
    n, block_ref, place_ref, offset_ref, q_hbm, k_hbm, v_hbm, out_ref,
    qbuf, kbuf, vbuf, masks, s0, s1, m0, m1, sbuf, mass_s, xbuf, mass_x, gbuf, mass_g, rbuf, mass_r, shares,
    kv_sem, q_local, q_send, q_recv, f_send, f_recv, x_send, x_recv, y_send, y_recv, r_send, r_recv, c_send, c_recv,
):
    me = lax.axis_index("seq")
    batch, _, rows, features = q_hbm.shape
    block = k_hbm.shape[1]
    shared = k_hbm.shape[2] // HEAD
    group = features // k_hbm.shape[2]
    top = block_ref.shape[1]
    tile = group * rows
    total = batch * tile
    chunks = block // CHUNK
    scores = (s0, s1)
    peaks = (m0, m1)

    lines = n // 2
    line, side = me // 2, lax.rem(me, 2)

    def device(j, p):
        return lax.rem(line + j, lines) * 2 + lax.rem(side + p, 2)

    loads = []
    for c in range(shared):
        columns = pl.ds(c * HEAD, HEAD)
        loads.append((
            pltpu.make_async_copy(k_hbm.at[0, :, columns], kbuf.at[c], kv_sem.at[0, c]),
            pltpu.make_async_copy(v_hbm.at[0, :, columns], vbuf.at[c], kv_sem.at[1, c]),
        ))
    own_query = pltpu.make_async_copy(q_hbm.at[:, 0], qbuf.at[0], q_local.at[0])
    own_query.start()
    for c in range(shared):
        loads[c][0].start()
    for c in range(shared):
        loads[c][1].start()

    barrier = pltpu.get_barrier_semaphore()

    def greet(target):
        pl.semaphore_signal(barrier, inc=1, device_id={"seq": target}, device_id_type=MESH)

    greet(device(0, 1))

    @pl.loop(1, lines)
    def _(j):
        greet(device(j, 0))

    pl.semaphore_wait(barrier, lines)

    def remote(src, dst, send, recv, target):
        return pltpu.make_async_remote_copy(
            src_ref=src, dst_ref=dst, send_sem=send, recv_sem=recv,
            device_id={"seq": target}, device_id_type=MESH)

    def query_copy(j, there):
        return remote(q_hbm.at[:, 0], qbuf.at[2 * there], q_send.at[j], q_recv.at[there], device(j, 0))

    def forward_copy(j):
        return remote(qbuf.at[2 * j], qbuf.at[2 * j + 1], f_send.at[j], f_recv.at[j], device(0, 1))

    def cross_copies(j):
        return (remote(sbuf.at[2 * j + 1], xbuf.at[j], x_send.at[j], x_recv.at[j], device(0, 1)),
                remote(mass_s.at[2 * j + 1], mass_x.at[j], y_send.at[j], y_recv.at[j], device(0, 1)))

    def return_copies(j, there):
        return (remote(gbuf.at[j], rbuf.at[there], r_send.at[j], r_recv.at[there], device(j, 0)),
                remote(mass_g.at[j], mass_r.at[there], c_send.at[j], c_recv.at[there], device(j, 0)))

    @pl.loop(1, lines)
    def _(j):
        query_copy(j, lines - j).start()

    own_query.wait()
    forward_copy(0).start()

    my_block = lax.fori_loop(
        0, place_ref.shape[0], lambda e, found: found + jnp.where(place_ref[e] == me, e, 0), jnp.int32(0))
    lanes = lax.broadcasted_iota(jnp.int32, (1, HEAD), 1)
    tile_lane = lax.broadcasted_iota(jnp.int32, (tile, HEAD), 1)
    tile_row = lax.rem(lax.broadcasted_iota(jnp.int32, (tile, HEAD), 0), rows)

    def first_hidden(d):
        hidden = jnp.zeros((1, HEAD), jnp.int32)
        for b in range(batch):
            t = b * n + device(d // 2, lax.rem(d, 2))
            entries = [block_ref[t, e] for e in range(top)]
            own = functools.reduce(jnp.maximum, entries)
            hits = functools.reduce(lambda x, y: x + y, [jnp.where(e == my_block, 1, 0) for e in entries])
            start = jnp.where(own == my_block, offset_ref[t] * rows, jnp.where(hits > 0, block, -2 * rows))
            column = lanes - b * rows
            hidden = jnp.where((column >= 0) & (column < rows), start + column + 1, hidden)
        return hidden

    def query_rows(d, c):
        parts = []
        for b in range(batch):
            piece = jnp.concatenate(
                [qbuf[d, b, :, pl.ds((c * group + g) * HEAD, HEAD)] for g in range(group)], axis=0)
            mark = jnp.where(tile_lane == tile_row + b * rows, MASKED, 0.0).astype(BF16)
            parts.append(jnp.concatenate([piece, mark], axis=1))
        return jnp.concatenate(parts, axis=0)

    def both(fresh, ready):
        if fresh is not None:
            d_new, c_new = fresh
            query = query_rows(d_new, c_new)
            peak = None
            if c_new == 0:
                hidden = first_hidden(d_new)
        if ready is not None:
            d_old, c_old = ready
            top_score = jnp.max(peaks[c_old][...], axis=1, keepdims=True)
            blend = jnp.zeros((total, 2 * HEAD), F32)
        for j in range(chunks):
            here = slice(j * CHUNK, (j + 1) * CHUNK)
            if fresh is not None:
                if c_new == 0:
                    position = lax.broadcasted_iota(jnp.int32, (CHUNK, HEAD), 0) + j * CHUNK
                    mask = jnp.where(position >= hidden, 1.0, 0.0).astype(BF16)
                    masks[here, :] = mask
                else:
                    mask = masks[here, :]
                part = dot_t(query, jnp.concatenate([kbuf[c_new, here, :], mask], axis=1))
                scores[c_new][:, here] = part
                for i in range(CHUNK // HEAD):
                    column = part[:, i * HEAD:(i + 1) * HEAD]
                    peak = column if peak is None else jnp.maximum(peak, column)
            if ready is not None:
                weights = jnp.exp2((scores[c_old][:, here] - top_score) * RATE).astype(BF16)
                value = jnp.concatenate([vbuf[c_old, here, :], jnp.ones((CHUNK, HEAD), BF16)], axis=1)
                blend = blend + jnp.dot(weights, value, preferred_element_type=F32)
        if fresh is not None:
            peaks[c_new][...] = peak
        if ready is not None:
            summed = blend[:, HEAD:]
            result = (blend[:, :HEAD] / summed).astype(BF16)
            mass = jnp.log2(summed) + top_score * RATE
            head_lane = lax.broadcasted_iota(jnp.int32, (rows, HEAD), 1)
            for b in range(batch):
                kept = jnp.zeros((rows, HEAD), F32) if c_old == 0 else mass_s[d_old, b]
                for g in range(group):
                    span = slice(b * tile + g * rows, b * tile + (g + 1) * rows)
                    head = c_old * group + g
                    sbuf[d_old, b, :, pl.ds(head * HEAD, HEAD)] = result[span]
                    kept = jnp.where(head_lane == head, mass[span], kept)
                mass_s[d_old, b] = kept

    for c in range(shared):
        loads[c][0].wait()
        loads[c][1].wait()
    both((0, 0), None)

    def merge(j):
        for copy in cross_copies(j):
            copy.wait_recv()
        for b in range(batch):
            mine, other = mass_s[2 * j, b], mass_x[j, b]
            highest = jnp.maximum(mine, other)
            first, second = jnp.exp2(mine - highest), jnp.exp2(other - highest)
            bottom = first + second
            mass_g[j, b] = highest + jnp.log2(bottom)
            first, second = first / bottom, second / bottom
            for head in range(shared * group):
                columns = pl.ds(head * HEAD, HEAD)
                gbuf[j, b, :, columns] = (
                    first[:, head:head + 1] * sbuf[2 * j, b, :, columns].astype(F32)
                    + second[:, head:head + 1] * xbuf[j, b, :, columns].astype(F32)).astype(BF16)

    def finish(j):
        merge(j)

        @pl.when(j > 0)
        def _():
            for copy in return_copies(j, lines - j):
                copy.start()

    def step(j, more):
        near, far = 2 * j, 2 * j + 1
        both((near, 1), (near, 0))
        forward_copy(j).wait_recv()
        both((far, 0), (near, 1))
        if more:
            query_copy(j + 1, j + 1).wait_recv()
            forward_copy(j + 1).start()
        both((far, 1), (far, 0))
        if more:
            @pl.when(j > 0)
            def _():
                finish(j - 1)
        elif lines > 1:
            finish(j - 1)
        both((2 * j + 2, 0) if more else None, (far, 1))
        for copy in cross_copies(j):
            copy.start()

    @pl.loop(0, lines - 1)
    def _(j):
        step(j, True)

    step(lines - 1, False)
    finish(lines - 1)

    @pl.loop(1, lines)
    def _(j):
        for copy in return_copies(j, j):
            copy.wait_recv()

    for_all = lambda f, init: lax.fori_loop(1, lines, f, init)
    highest = for_all(lambda j, m: jnp.maximum(m, mass_r[j]), mass_g[0])
    bottom = for_all(lambda j, total_: total_ + jnp.exp2(mass_r[j] - highest), jnp.exp2(mass_g[0] - highest))
    shares[0] = jnp.exp2(mass_g[0] - highest) / bottom

    @pl.loop(1, lines)
    def _(j):
        shares[j] = jnp.exp2(mass_r[j] - highest) / bottom

    for b in range(batch):
        for head in range(shared * group):
            columns = pl.ds(head * HEAD, HEAD)

            def add(j, sofar):
                return sofar + shares[j, b][:, head:head + 1] * rbuf[j, b, :, columns].astype(F32)

            value = shares[0, b][:, head:head + 1] * gbuf[0, b, :, columns].astype(F32)
            out_ref[b, 0, :, columns] = lax.fori_loop(1, lines, add, value, unroll=n <= 8).astype(BF16)

    @pl.loop(0, lines)
    def _(j):
        forward_copy(j).wait_send()
        for copy in cross_copies(j):
            copy.wait_send()

    @pl.loop(1, lines)
    def _(j):
        query_copy(j, j).wait_send()
        for copy in return_copies(j, j):
            copy.wait_send()


def local(n, queries, keys, values, tile_blocks, block_place, tile_offset):
    batch, _, rows, features = queries.shape
    block = keys.shape[1]
    shared = keys.shape[2] // HEAD
    group = features // keys.shape[2]
    total = batch * group * rows
    lines = n // 2
    smem = pl.BlockSpec(memory_space=pltpu.SMEM)
    far = pl.BlockSpec(memory_space=pl.ANY)
    dma = pltpu.SemaphoreType.DMA
    return pl.pallas_call(
        functools.partial(kernel, n),
        out_shape=jax.ShapeDtypeStruct(queries.shape, queries.dtype),
        in_specs=[smem, smem, smem, far, far, far],
        out_specs=pl.BlockSpec(memory_space=pltpu.VMEM),
        scratch_shapes=[
            pltpu.VMEM((n, batch, rows, features), BF16),
            pltpu.VMEM((shared, block, HEAD), BF16),
            pltpu.VMEM((shared, block, HEAD), BF16),
            pltpu.VMEM((block, HEAD), BF16),
            pltpu.VMEM((total, block), F32),
            pltpu.VMEM((total, block), F32),
            pltpu.VMEM((total, HEAD), F32),
            pltpu.VMEM((total, HEAD), F32),
            pltpu.VMEM((n, batch, rows, features), BF16),
            pltpu.VMEM((n, batch, rows, HEAD), F32),
            pltpu.VMEM((lines, batch, rows, features), BF16),
            pltpu.VMEM((lines, batch, rows, HEAD), F32),
            pltpu.VMEM((lines, batch, rows, features), BF16),
            pltpu.VMEM((lines, batch, rows, HEAD), F32),
            pltpu.VMEM((lines, batch, rows, features), BF16),
            pltpu.VMEM((lines, batch, rows, HEAD), F32),
            pltpu.VMEM((lines, batch, rows, HEAD), F32),
            dma((2, shared)),
            dma((1,)),
            *[dma((lines,))] * 12,
        ],
        compiler_params=pltpu.CompilerParams(
            collective_id=0, has_side_effects=True, vmem_limit_bytes=60 * 1024 * 1024),
    )(tile_blocks, block_place, tile_offset, queries, keys, values)


def solution(mesh):
    placed = (
        P(None, ("groups", "seq"), None, "heads"),
        P(("groups", "seq"), None, "heads"),
        P(("groups", "seq"), None, "heads"),
        P("groups", None),
        P("groups"),
        P("groups"),
    )
    return jax.shard_map(
        functools.partial(local, mesh.shape["seq"]),
        mesh=mesh,
        in_specs=placed,
        out_specs=P(None, ("groups", "seq"), None, "heads"),
        check_vma=False,
    )
```
